32 devices in a mesh: parts: 2 (over x), outer: 8 (over z, y), inner: 2 (over core).
Axes of the slice: x: 2, y: 2, z: 4, core: 2. Of those that a mesh axis runs over, the one named last changes fastest.
Arguments:
- state: float32 [2, 8388608], P(None, ('parts', 'outer', 'inner')), parts along dimension 1, may hold values from -6 to 6
- gates: bfloat16 [8, 2, 128, 128], replicated, may hold values from -0.375 to 0.375
- bonds: float32 [8, 2, 2, 128], replicated, may hold values from -4 to 4
- order: int32 [8], replicated, may hold values from 0 to 7, each once
- slice_bits: int32 [16], P('parts'), parts along dimension 0, may hold values from 0 to 1
Outputs:
- result: float32 [2, 8388608], P(None, ('parts', 'outer', 'inner')), parts along dimension 1
The draws below stay inside these ranges and needn't reach their ends.
There are 2 independent parts, one for each index of `parts`. The reference program is written for one: setup_inputs(seed, part) draws one part's arguments, and reference() takes and returns one part's arrays. A program takes and returns all parts, laid end to end along the dimension named above; an argument that names none is the same for every part. Nothing has to cross between parts.
Inputs may be any that keep to these rules, and one draw needn't show every extreme that they name: `order`: each branch matrix is named once.
All inputs are finite; a program needn't handle non-finite values.
Results may differ from the reference program's by a relative error of at most 0.0003.
Values sent between devices are 32-bit elements; how exact they have to be, the bound alone decides.
No kernel may reach another device: no remote copies, remote signals or barrier semaphores. Data moves between devices by JAX's collectives and lax.ppermute only.
A program may use at most 64 MiB of HBM per device.

```python
import jax
import jax.numpy as jnp
from jax import lax

AMP_DEV = 262144
ORDER_DIM = 128
BRANCHES = 8
LEAD = 8
SECOND = 2
AMPS = 4194304


def set_ends(array, rng, smallest, largest):
    longest = array.shape.index(max(array.shape))
    spots = []
    for shift in (0, 1):
        where = [jax.random.randint(jax.random.fold_in(rng, axis), (), 0, length) for axis, length in enumerate(array.shape)]
        where[longest] = (where[longest] + shift) % array.shape[longest]
        spots.append(tuple(where))
    return array.at[spots[0]].set(smallest).at[spots[1]].set(largest)


def steps_of(stream_key, extent, cuts, low, largest):
    loudness = 1.0
    for axis_at, blocks in cuts:
        steps = jax.random.uniform(jax.random.fold_in(jax.random.fold_in(stream_key, 6), axis_at), (blocks,), jnp.float32, low / len(cuts), largest / len(cuts))
        loudness = loudness * jnp.repeat(jnp.exp(steps), extent[axis_at] // blocks).reshape((-1,) + (1,) * (len(extent) - 1 - axis_at))
    return loudness


def centred(key, dims, spread, reach, cuts=(), held_as=jnp.bfloat16):
    loudness = steps_of(key, dims, cuts, -0.22, 0.18) if cuts else 1.0
    values = jax.random.normal(key, dims, jnp.float32) * spread * loudness
    return jnp.minimum(jnp.maximum(values, -reach), reach).astype(held_as)


def setup_inputs(seed: int = 0, part: int = 0) -> dict:
    keys = jax.random.split(jax.random.key(seed), 6)
    own_keys = jax.random.split(jax.random.fold_in(keys[5], part), 6)
    state = centred(own_keys[0], (2, AMPS), 1.0, 6.0, ((1, 16),), jnp.float32)
    gates = centred(keys[1], (BRANCHES, 2, ORDER_DIM, ORDER_DIM), (2 * ORDER_DIM) ** -0.5, 0.375)
    bonds = centred(keys[2], (BRANCHES, 2, 2, ORDER_DIM), 0.7071, 4.0, (), jnp.float32)
    order = jax.random.permutation(keys[3], BRANCHES).astype(jnp.int32)
    slice_bits = set_ends(jax.random.randint(own_keys[4], (BRANCHES,), 0, 2), jax.random.fold_in(own_keys[4], 1), 0, 1).astype(jnp.int32)
    return {"state": state, "gates": gates, "bonds": bonds, "order": order, "slice_bits": slice_bits}


def build_branch(gates, bonds, order, slice_bits, step):
    matrix = gates[order[step]].astype(jnp.float32)
    factor = bonds[order[step], slice_bits[step]]
    real_branch = matrix[0] * factor[0][None, :] - matrix[1] * factor[1][None, :]
    imag_branch = matrix[0] * factor[1][None, :] + matrix[1] * factor[0][None, :]
    return jnp.stack([real_branch, imag_branch])


def contract_all(psi, branch):
    groups = psi.shape[1]
    viewed = psi.reshape(2, groups, 128, -1)
    real_part = viewed[0]
    imag_part = viewed[1]
    high = lax.Precision.HIGHEST
    real_out = jnp.einsum('gbj,ab->gja', real_part, branch[0], precision=high) - jnp.einsum('gbj,ab->gja', imag_part, branch[1], precision=high)
    imag_out = jnp.einsum('gbj,ab->gja', real_part, branch[1], precision=high) + jnp.einsum('gbj,ab->gja', imag_part, branch[0], precision=high)
    return jnp.stack([real_out.reshape(groups, -1), imag_out.reshape(groups, -1)])


def reference(state, gates, bonds, order, slice_bits):
    psi = state.reshape(2, LEAD * SECOND, AMP_DEV)
    for step in range(3):
        psi = contract_all(psi, build_branch(gates, bonds, order, slice_bits, step))
    psi = psi.reshape(2, LEAD, SECOND, LEAD, AMP_DEV // LEAD)
    psi = jnp.transpose(psi, (0, 3, 2, 1, 4)).reshape(2, LEAD * SECOND, AMP_DEV)
    for step in range(3, 6):
        psi = contract_all(psi, build_branch(gates, bonds, order, slice_bits, step))
    psi = psi.reshape(2, LEAD, SECOND, SECOND, AMP_DEV // SECOND)
    psi = jnp.transpose(psi, (0, 1, 3, 2, 4)).reshape(2, LEAD * SECOND, AMP_DEV)
    for step in range(6, 8):
        psi = contract_all(psi, build_branch(gates, bonds, order, slice_bits, step))
    return psi.reshape(2, AMPS)
```

```python
import functools

import jax
import jax.numpy as jnp
from jax import lax
from jax.experimental import pallas as pl
from jax.experimental.pallas import tpu as pltpu
from jax.sharding import PartitionSpec as P

UNROLL = 8


def build_weights(gate_ref, weight_ref):
    dim = gate_ref.shape[-1]
    real = gate_ref[0, 0].astype(jnp.float32).T.astype(jnp.bfloat16)
    imag = gate_ref[0, 1].astype(jnp.float32).T.astype(jnp.bfloat16)
    weight_ref[:dim, :dim] = real
    weight_ref[:dim, dim:] = imag
    weight_ref[dim:, :dim] = -imag
    weight_ref[dim:, dim:] = real


def contract(load, store, weight_ref, bond_ref, groups):
    bond_real = bond_ref[0, 0, 0:1, :]
    bond_imag = bond_ref[0, 0, 1:2, :]
    unroll = min(UNROLL, groups)

    def some(index, carry):
        high, low = [], []
        for k in range(unroll):
            real, imag = load(index * unroll + k)
            real, imag = real.T, imag.T
            scaled = jnp.concatenate(
                [real * bond_real - imag * bond_imag, real * bond_imag + imag * bond_real], axis=1
            )
            head = scaled.astype(jnp.bfloat16)
            high.append(head)
            low.append((scaled - head.astype(jnp.float32)).astype(jnp.bfloat16))
        product = jnp.dot(
            jnp.concatenate(high + low, axis=0), weight_ref[...], preferred_element_type=jnp.float32
        )
        half = product.shape[0] // 2
        product = product[:half] + product[half:]
        size = half // unroll
        for k in range(unroll):
            store(index * unroll + k, product[k * size : (k + 1) * size])
        return carry

    lax.fori_loop(0, groups // unroll, some, 0)


def kernel(order_ref, bits_ref, *refs, steps, n_in, n_out, in_axis, out_axis, rows):
    del order_ref, bits_ref
    refs = list(refs)
    ins = [refs.pop(0) for _ in range(n_in)]
    gates = [refs.pop(0) for _ in range(steps)]
    bonds = [refs.pop(0) for _ in range(steps)]
    outs = [refs.pop(0) for _ in range(n_out)]
    weight_ref, bufs, in_sem, out_sem = refs
    dim = weight_ref.shape[-1] // 2
    groups = rows // dim

    if in_axis is not None:
        me = lax.axis_index(in_axis)
        part = rows // n_in
        copies = []
        for k in range(n_in):
            start = pl.multiple_of(lax.rem(me + (n_in - k), n_in) * part, part)
            for c in range(2):
                copies.append(
                    pltpu.make_async_copy(
                        ins[k].at[c], bufs.at[0, c, pl.ds(start, part), :], in_sem.at[k, c]
                    )
                )
                copies[-1].start()

    for s in range(steps):
        build_weights(gates[s], weight_ref.at[s])
    if in_axis is not None:
        for copy in copies:
            copy.wait()

    def load_interleaved(g):
        return tuple(ins[0][pl.ds(2 * g + c, dim, stride=2 * groups), :] for c in range(2))

    def loader(which):
        def load(g):
            return tuple(bufs[which, c, pl.ds(g, dim, stride=groups), :] for c in range(2))

        return load

    def storer(which):
        def store(g, value):
            for c in range(2):
                bufs[which, c, pl.ds(pl.multiple_of(g * dim, dim), dim), :] = value[
                    :, c * dim : (c + 1) * dim
                ]

        return store

    def store_interleaved(g, value):
        for c in range(2):
            outs[0][pl.ds(2 * g * dim + c, dim, stride=2), :] = value[:, c * dim : (c + 1) * dim]

    for s in range(steps):
        load = load_interleaved if in_axis is None and s == 0 else loader(s % 2)
        last = out_axis is None and s == steps - 1
        store = store_interleaved if last else storer((s + 1) % 2)
        contract(load, store, weight_ref.at[s], bonds[s], groups)

    if out_axis is not None:
        me = lax.axis_index(out_axis)
        part = rows // n_out
        copies = []
        for k in range(n_out):
            start = pl.multiple_of(lax.rem(me + k, n_out) * part, part)
            for c in range(2):
                copies.append(
                    pltpu.make_async_copy(
                        bufs.at[steps % 2, c, pl.ds(start, part), :], outs[k].at[c], out_sem.at[k, c]
                    )
                )
                copies[-1].start()
        for copy in copies:
            copy.wait()


def call(ins, gates, bonds, order, bits, first, steps, rows, n_out, in_axis, out_axis):
    dim = gates.shape[-1]
    n_in = len(ins)

    def gate_map(k, i, order, bits):
        return (order[first + k], 0, 0, 0)

    def bond_map(k, i, order, bits):
        return (order[first + k], bits[first + k], 0, 0)

    anywhere = pl.BlockSpec(memory_space=pl.ANY)
    flat = pl.BlockSpec((2 * rows, dim), lambda i, order, bits: (0, 0))
    in_specs = [flat] if in_axis is None else [anywhere] * n_in
    in_specs += [
        pl.BlockSpec((1,) + gates.shape[1:], functools.partial(gate_map, k)) for k in range(steps)
    ]
    in_specs += [
        pl.BlockSpec((1, 1) + bonds.shape[2:], functools.partial(bond_map, k)) for k in range(steps)
    ]
    if out_axis is None:
        out_shape = [jax.ShapeDtypeStruct((2 * rows, dim), jnp.float32)]
        out_specs = [flat]
    else:
        out_shape = [jax.ShapeDtypeStruct((2, rows // n_out, dim), jnp.float32)] * n_out
        out_specs = [anywhere] * n_out
    return pl.pallas_call(
        functools.partial(
            kernel,
            steps=steps,
            n_in=n_in,
            n_out=n_out,
            in_axis=in_axis,
            out_axis=out_axis,
            rows=rows,
        ),
        out_shape=out_shape,
        grid_spec=pltpu.PrefetchScalarGridSpec(
            num_scalar_prefetch=2,
            grid=(1,),
            in_specs=in_specs,
            out_specs=out_specs,
            scratch_shapes=[
                pltpu.VMEM((steps, 2 * dim, 2 * dim), jnp.bfloat16),
                pltpu.VMEM((2, 2, rows, dim), jnp.float32),
                pltpu.SemaphoreType.DMA((n_in, 2)),
                pltpu.SemaphoreType.DMA((n_out, 2)),
            ],
        ),
        cost_estimate=pl.CostEstimate(
            flops=steps * 16 * rows * dim * dim, bytes_accessed=16 * rows * dim, transcendentals=0
        ),
    )(order, bits, *ins, *([gates] * steps), *([bonds] * steps))


def exchange(pieces, axis):
    n = len(pieces)
    return [pieces[0]] + [
        lax.ppermute(pieces[k], axis, [(i, (i + k) % n) for i in range(n)]) for k in range(1, n)
    ]


def body(state, gates, bonds, order, bits):
    dim = gates.shape[-1]
    rows = state.shape[1] // dim
    leading = lax.axis_size("outer")
    second = lax.axis_size("inner")
    flat = state.reshape(2, rows, dim).transpose(1, 0, 2).reshape(2 * rows, dim)
    run = functools.partial(call, gates=gates, bonds=bonds, order=order, bits=bits, rows=rows)
    pieces = run([flat], first=0, steps=3, n_out=leading, in_axis=None, out_axis="outer")
    pieces = exchange(pieces, "outer")
    pieces = run(pieces, first=3, steps=3, n_out=second, in_axis="outer", out_axis="inner")
    pieces = exchange(pieces, "inner")
    (flat,) = run(pieces, first=6, steps=2, n_out=1, in_axis="inner", out_axis=None)
    return flat.reshape(rows, 2, dim).transpose(1, 0, 2).reshape(2, rows * dim)


def solution(mesh):
    in_specs = (P(None, ("parts", "outer", "inner")), P(), P(), P(), P("parts"))
    out_specs = P(None, ("parts", "outer", "inner"))
    return jax.shard_map(body, mesh=mesh, in_specs=in_specs, out_specs=out_specs, check_vma=False)
```

```python
import functools

import jax
import jax.numpy as jnp
from jax import lax
from jax.experimental import pallas as pl
from jax.experimental.pallas import tpu as pltpu
from jax.sharding import PartitionSpec as P


UNROLL = 8


def build_weights(gate_ref, weight_ref):
    dim = gate_ref.shape[-1]
    real = gate_ref[0, 0].astype(jnp.float32).T.astype(jnp.bfloat16)
    imag = gate_ref[0, 1].astype(jnp.float32).T.astype(jnp.bfloat16)
    weight_ref[:dim, :dim] = real
    weight_ref[:dim, dim:] = imag
    weight_ref[dim:, :dim] = -imag
    weight_ref[dim:, dim:] = real


def contract(load, store, weight_ref, bond_ref, groups):
    bond_real = bond_ref[0, 0, 0:1, :]
    bond_imag = bond_ref[0, 0, 1:2, :]
    unroll = min(UNROLL, groups)

    def some(index, carry):
        high, low = [], []
        for k in range(unroll):
            real, imag = load(index * unroll + k)
            real, imag = real.T, imag.T
            scaled = jnp.concatenate(
                [real * bond_real - imag * bond_imag, real * bond_imag + imag * bond_real], axis=1
            )
            head = scaled.astype(jnp.bfloat16)
            high.append(head)
            low.append((scaled - head.astype(jnp.float32)).astype(jnp.bfloat16))
        product = jnp.dot(
            jnp.concatenate(high + low, axis=0), weight_ref[...], preferred_element_type=jnp.float32
        )
        half = product.shape[0] // 2
        product = product[:half] + product[half:]
        size = half // unroll
        for k in range(unroll):
            store(index * unroll + k, product[k * size : (k + 1) * size])
        return carry

    lax.fori_loop(0, groups // unroll, some, 0)


def kernel(order_ref, bits_ref, *refs, steps, n_in, n_out, in_axis, out_axis, rows):
    del order_ref, bits_ref
    refs = list(refs)
    ins = [refs.pop(0) for _ in range(n_in)]
    gates = [refs.pop(0) for _ in range(steps)]
    bonds = [refs.pop(0) for _ in range(steps)]
    outs = [refs.pop(0) for _ in range(n_out)]
    weight_ref, bufs, in_sem, out_sem = refs
    dim = weight_ref.shape[-1] // 2
    groups = rows // dim

    if in_axis is not None:
        me = lax.axis_index(in_axis)
        part = rows // n_in
        copies = []
        for k in range(n_in):
            start = pl.multiple_of(lax.rem(me + (n_in - k), n_in) * part, part)
            for c in range(2):
                copies.append(
                    pltpu.make_async_copy(
                        ins[k].at[c], bufs.at[0, c, pl.ds(start, part), :], in_sem.at[k, c]
                    )
                )
                copies[-1].start()

    for s in range(steps):
        build_weights(gates[s], weight_ref.at[s])
    if in_axis is not None:
        for copy in copies:
            copy.wait()

    def load_interleaved(g):
        return tuple(ins[0][pl.ds(2 * g + c, dim, stride=2 * groups), :] for c in range(2))

    def loader(which):
        def load(g):
            return tuple(bufs[which, c, pl.ds(g, dim, stride=groups), :] for c in range(2))

        return load

    def storer(which):
        def store(g, value):
            for c in range(2):
                bufs[which, c, pl.ds(pl.multiple_of(g * dim, dim), dim), :] = value[
                    :, c * dim : (c + 1) * dim
                ]

        return store

    def store_interleaved(g, value):
        for c in range(2):
            outs[0][pl.ds(2 * g * dim + c, dim, stride=2), :] = value[:, c * dim : (c + 1) * dim]

    for s in range(steps):
        load = load_interleaved if in_axis is None and s == 0 else loader(s % 2)
        last = out_axis is None and s == steps - 1
        store = store_interleaved if last else storer((s + 1) % 2)
        contract(load, store, weight_ref.at[s], bonds[s], groups)

    if out_axis is not None:
        me = lax.axis_index(out_axis)
        part = rows // n_out
        copies = []
        for k in range(n_out):
            start = pl.multiple_of(lax.rem(me + k, n_out) * part, part)
            for c in range(2):
                copies.append(
                    pltpu.make_async_copy(
                        bufs.at[steps % 2, c, pl.ds(start, part), :], outs[k].at[c], out_sem.at[k, c]
                    )
                )
                copies[-1].start()
        for copy in copies:
            copy.wait()


def call(ins, gates, bonds, order, bits, first, steps, rows, n_out, in_axis, out_axis):
    dim = gates.shape[-1]
    n_in = len(ins)

    def gate_map(k, i, order, bits):
        return (order[first + k], 0, 0, 0)

    def bond_map(k, i, order, bits):
        return (order[first + k], bits[first + k], 0, 0)

    anywhere = pl.BlockSpec(memory_space=pl.ANY)
    flat = pl.BlockSpec((2 * rows, dim), lambda i, order, bits: (0, 0))
    in_specs = [flat] if in_axis is None else [anywhere] * n_in
    in_specs += [
        pl.BlockSpec((1,) + gates.shape[1:], functools.partial(gate_map, k)) for k in range(steps)
    ]
    in_specs += [
        pl.BlockSpec((1, 1) + bonds.shape[2:], functools.partial(bond_map, k)) for k in range(steps)
    ]
    if out_axis is None:
        out_shape = [jax.ShapeDtypeStruct((2 * rows, dim), jnp.float32)]
        out_specs = [flat]
    else:
        out_shape = [jax.ShapeDtypeStruct((2, rows // n_out, dim), jnp.float32)] * n_out
        out_specs = [anywhere] * n_out
    return pl.pallas_call(
        functools.partial(
            kernel,
            steps=steps,
            n_in=n_in,
            n_out=n_out,
            in_axis=in_axis,
            out_axis=out_axis,
            rows=rows,
        ),
        out_shape=out_shape,
        grid_spec=pltpu.PrefetchScalarGridSpec(
            num_scalar_prefetch=2,
            grid=(1,),
            in_specs=in_specs,
            out_specs=out_specs,
            scratch_shapes=[
                pltpu.VMEM((steps, 2 * dim, 2 * dim), jnp.bfloat16),
                pltpu.VMEM((2, 2, rows, dim), jnp.float32),
                pltpu.SemaphoreType.DMA((n_in, 2)),
                pltpu.SemaphoreType.DMA((n_out, 2)),
            ],
        ),
        cost_estimate=pl.CostEstimate(
            flops=steps * 16 * rows * dim * dim, bytes_accessed=16 * rows * dim, transcendentals=0
        ),
    )(order, bits, *ins, *([gates] * steps), *([bonds] * steps))


def exchange(pieces, axis):
    n = len(pieces)
    return [pieces[0]] + [
        lax.ppermute(pieces[k], axis, [(i, (i + k) % n) for i in range(n)]) for k in range(1, n)
    ]


def general_body(state, gates, bonds, order, bits):
    dim = gates.shape[-1]
    rows = state.shape[1] // dim
    leading = lax.axis_size("outer")
    second = lax.axis_size("inner")
    flat = state.reshape(2, rows, dim).transpose(1, 0, 2).reshape(2 * rows, dim)
    run = functools.partial(call, gates=gates, bonds=bonds, order=order, bits=bits, rows=rows)
    pieces = run([flat], first=0, steps=3, n_out=leading, in_axis=None, out_axis="outer")
    pieces = exchange(pieces, "outer")
    pieces = run(pieces, first=3, steps=3, n_out=second, in_axis="outer", out_axis="inner")
    pieces = exchange(pieces, "inner")
    (flat,) = run(pieces, first=6, steps=2, n_out=1, in_axis="inner", out_axis=None)
    return flat.reshape(rows, 2, dim).transpose(1, 0, 2).reshape(2, rows * dim)


VMEM_LIMIT = 20 * 2**20


def gate_rows(gate_ref, scratch_ref, order):
    for c in range(2):
        scratch_ref[c] = gate_ref[c].astype(jnp.float32)
    if order is None:
        return [scratch_ref[c] for c in range(2)]
    tall = scratch_ref.shape[1] // len(order)
    return [
        jnp.concatenate([scratch_ref[c, pl.ds(t, tall, stride=len(order)), :] for t in order], axis=0)
        for c in range(2)
    ]


def make_weight(gate_ref, scratch_ref, weight_ref, order=None, halves=False):
    real, imag = gate_rows(gate_ref, scratch_ref, order)
    dim = real.shape[0]
    cut = [(0, dim // 2), (dim // 2, dim)] if halves else [(0, dim)]
    upper = [m[a:b] for a, b in cut for m in (real, imag)]
    lower = [m[a:b] for a, b in cut for m in (-imag, real)]
    weight_ref[:dim] = jnp.concatenate(upper, axis=0).T.astype(jnp.bfloat16)
    weight_ref[dim:] = jnp.concatenate(lower, axis=0).T.astype(jnp.bfloat16)


def apply_gate(load, store, weight_ref, bond_ref, groups, unroll):
    bond_real = bond_ref[0:1, :]
    bond_imag = bond_ref[1:2, :]

    def some(index, carry):
        high, low = [], []
        for k in range(unroll):
            tiles = load(index * unroll + k)
            if len(tiles) == 1:
                both = tiles[0].T
                half = both.shape[0] // 2
                real, imag = both[:half], both[half:]
            else:
                real, imag = tiles[0].T, tiles[1].T
            scaled = jnp.concatenate(
                [real * bond_real - imag * bond_imag, real * bond_imag + imag * bond_real], axis=1
            )
            head = scaled.astype(jnp.bfloat16)
            high.append(head)
            low.append((scaled - head.astype(jnp.float32)).astype(jnp.bfloat16))
        product = jnp.dot(
            jnp.concatenate(high + low, axis=0), weight_ref[...], preferred_element_type=jnp.float32
        )
        half = product.shape[0] // 2
        product = product[:half] + product[half:]
        size = half // unroll
        for k in range(unroll):
            store(index * unroll + k, product[k * size : (k + 1) * size])
        return carry

    lax.fori_loop(0, groups // unroll, some, 0)


def tiles_of(ref, lead=()):
    def load(g):
        value = ref[(*lead, slice(None), pl.ds(pl.multiple_of(g * 8, 8), 8), slice(None))]
        return value.reshape(-1, value.shape[-1])

    return load


def parts_of(ref):
    loads = [tiles_of(ref, (c,)) for c in range(2)]
    return lambda g: [load(g) for load in loads]


def fetch(order_ref, bits_ref, first, gates_ref, bonds_ref, gate_buf, bond_buf, sem):
    copies = []
    for k in range(gate_buf.shape[0]):
        which = order_ref[first + k]
        copies.append(pltpu.make_async_copy(gates_ref.at[which], gate_buf.at[k], sem.at[k, 0]))
        copies.append(
            pltpu.make_async_copy(bonds_ref.at[which, bits_ref[first + k]], bond_buf.at[k], sem.at[k, 1])
        )
    for copy in copies:
        copy.start()
    return copies


def start_all(copies):
    for copy in copies:
        copy.start()
    return copies


def wait_all(copies):
    for copy in copies:
        copy.wait()


def second_third(half, d1, out_buf, outs, weights, bonds, sem):
    groups = d1.shape[1]

    def load(g):
        return [half[pl.ds(g, half.shape[1], stride=groups), :]]

    def store(g, value):
        lanes = half.shape[1]
        for c in range(2):
            d1[c, g] = value[:, c * lanes : (c + 1) * lanes]

    apply_gate(load, store, weights.at[0], bonds.at[0], groups, 8)
    per = out_buf.shape[1] // len(outs)

    def store_out(g, value):
        lanes = half.shape[1]
        for c in range(2):
            out_buf[c, g] = value[:, c * lanes : (c + 1) * lanes]

    apply_gate(parts_of(d1), store_out, weights.at[1], bonds.at[1], out_buf.shape[1], 8)
    wait_all(
        start_all(
            [
                pltpu.make_async_copy(out_buf.at[:, pl.ds(k * per, per)], outs[k], sem.at[k])
                for k in range(len(outs))
            ]
        )
    )


def head_kernel(order_ref, bits_ref, x_ref, gates_ref, bonds_ref, *refs, n):
    far_outs, near_ref = refs[: n // 2], refs[n // 2]
    x_buf, far, near, d1, out_buf, gate_buf, bond_buf, gate_rows_buf, weights, g_sem, x_sem, o_sem, n_sem = refs[
        n // 2 + 1 :
    ]
    groups = x_buf.shape[1]
    me = lax.axis_index("outer")
    gate_copies = fetch(order_ref, bits_ref, 0, gates_ref, bonds_ref, gate_buf, bond_buf, g_sem)

    def x_copy(g, c):
        return pltpu.make_async_copy(x_ref.at[:, g, c, :], x_buf.at[c, g], x_sem.at[c, g])

    for g in range(groups):
        for c in range(2):
            x_copy(g, c).start()
    wait_all(gate_copies)
    rest = groups // n
    leads = [(me ^ k) * rest + r for k in [*range(n // 2, n), *range(n // 2)] for r in range(rest)]
    tiles = list(range(groups))
    make_weight(gate_buf.at[0], gate_rows_buf, weights.at[0], leads, True)
    make_weight(gate_buf.at[1], gate_rows_buf, weights.at[1], tiles)
    make_weight(gate_buf.at[2], gate_rows_buf, weights.at[2], tiles, True)

    def load(g):
        for c in range(2):
            x_copy(g, c).wait()
        return [x_buf[c, g] for c in range(2)]

    def store(g, value):
        lanes = far.shape[1]
        rows = pl.ds(pl.multiple_of(g * lanes, lanes), lanes)
        far[rows, :] = value[:, :lanes]
        near[rows, :] = value[:, lanes:]

    apply_gate(load, store, weights.at[0], bond_buf.at[0], groups, 8)
    near_copy = pltpu.make_async_copy(near, near_ref, n_sem)
    near_copy.start()
    second_third(far, d1, out_buf, far_outs, weights.at[pl.ds(1, 2)], bond_buf.at[pl.ds(1, 2)], o_sem)
    near_copy.wait()


def near_kernel(order_ref, bits_ref, near_ref, gates_ref, bonds_ref, *refs, n):
    outs = refs[: n // 2]
    near, d1, out_buf, gate_buf, bond_buf, gate_rows_buf, weights, g_sem, o_sem, n_sem = refs[n // 2 :]
    near_copy = pltpu.make_async_copy(near_ref, near, n_sem)
    near_copy.start()
    wait_all(fetch(order_ref, bits_ref, 1, gates_ref, bonds_ref, gate_buf, bond_buf, g_sem))
    tiles = list(range(d1.shape[1]))
    make_weight(gate_buf.at[0], gate_rows_buf, weights.at[0], tiles)
    make_weight(gate_buf.at[1], gate_rows_buf, weights.at[1], tiles, True)
    near_copy.wait()
    second_third(near, d1, out_buf, outs, weights, bond_buf, o_sem)


def join_kernel(order_ref, bits_ref, gates_ref, bonds_ref, *refs, n):
    ins, (own_ref, other_ref) = refs[:n], refs[n : n + 2]
    v_buf, own, other, gate_buf, bond_buf, gate_rows_buf, weights, g_sem, i_sem, o_sem = refs[n + 2 :]
    me = lax.axis_index("outer")
    core = lax.axis_index("inner")
    per = ins[0].shape[1]
    copies = fetch(order_ref, bits_ref, 3, gates_ref, bonds_ref, gate_buf, bond_buf, g_sem)
    in_copies = start_all(
        [
            pltpu.make_async_copy(ins[k], v_buf.at[:, pl.ds((me ^ k) * per, per)], i_sem.at[k])
            for k in range(n)
        ]
    )
    wait_all(copies)
    groups = v_buf.shape[1]
    leads = [(core ^ j) * (groups // 2) + r for j in range(2) for r in range(groups // 2)]
    make_weight(gate_buf.at[0], gate_rows_buf, weights.at[0], leads, True)
    wait_all(in_copies)
    lanes = v_buf.shape[-1]
    out_copies = []
    for chunk in range(2):

        def load(g):
            return [tiles_of(v_buf, (chunk,))(g)]

        def store(g, value):
            own[chunk, g] = value[:, :lanes]
            other[chunk, g] = value[:, lanes:]

        apply_gate(load, store, weights.at[0], bond_buf.at[0], groups, 8)
        out_copies += start_all(
            [
                pltpu.make_async_copy(other.at[chunk], other_ref.at[chunk], o_sem.at[1, chunk]),
                pltpu.make_async_copy(own.at[chunk], own_ref.at[chunk], o_sem.at[0, chunk]),
            ]
        )
    wait_all(out_copies)


def fifth_sixth(q_buf, e_buf, s_buf, at, weights, bonds):
    lanes = q_buf.shape[-1]
    per = q_buf.shape[2] // 8
    for chunk in range(2):

        def load(g):
            return [tiles_of(q_buf, (chunk,))(g)]

        def store(g, value):
            for c in range(2):
                e_buf[c, chunk * per + g] = value[:, c * lanes : (c + 1) * lanes]

        apply_gate(load, store, weights.at[0], bonds.at[0], per, per)

    def store_s(g, value):
        for c in range(2):
            s_buf[c, at + g] = value[:, c * lanes : (c + 1) * lanes]

    groups = e_buf.shape[2] // 8
    apply_gate(parts_of(e_buf), store_s, weights.at[1], bonds.at[1], groups, groups)


def own_kernel(order_ref, bits_ref, own_ref, gates_ref, bonds_ref, out_ref, *refs):
    q_buf, e_buf, s_buf, gate_buf, bond_buf, gate_rows_buf, weights, g_sem, i_sem, o_sem = refs
    copy = pltpu.make_async_copy(own_ref, q_buf, i_sem)
    copy.start()
    wait_all(fetch(order_ref, bits_ref, 4, gates_ref, bonds_ref, gate_buf, bond_buf, g_sem))
    tiles = list(range(e_buf.shape[1]))
    for k in range(2):
        make_weight(gate_buf.at[k], gate_rows_buf, weights.at[k], tiles)
    copy.wait()
    fifth_sixth(q_buf, e_buf, s_buf, 0, weights, bond_buf)
    copy = pltpu.make_async_copy(s_buf, out_ref, o_sem)
    copy.start()
    copy.wait()


def tail_kernel(order_ref, bits_ref, done_ref, got_ref, gates_ref, bonds_ref, out_ref, *refs):
    q_buf, e_buf, s_buf, f_buf, y_buf, gate_buf, bond_buf, gate_rows_buf, weights, g_sem, i_sem, y_sem = refs
    core = lax.axis_index("inner")
    half = s_buf.shape[1] // 2
    got = pltpu.make_async_copy(got_ref, q_buf, i_sem.at[0])
    got.start()
    done = pltpu.make_async_copy(done_ref, s_buf.at[:, pl.ds(core * half, half)], i_sem.at[1])
    done.start()
    wait_all(fetch(order_ref, bits_ref, 4, gates_ref, bonds_ref, gate_buf, bond_buf, g_sem))
    tiles = list(range(e_buf.shape[1]))
    for k in range(4):
        make_weight(gate_buf.at[k], gate_rows_buf, weights.at[k], tiles if k < 2 else None)
    got.wait()
    fifth_sixth(q_buf, e_buf, s_buf, (1 - core) * half, weights, bond_buf)
    done.wait()
    lanes = f_buf.shape[-1]
    groups = f_buf.shape[1]

    def store(g, value):
        for c in range(2):
            f_buf[c, g] = value[:, c * lanes : (c + 1) * lanes]

    apply_gate(parts_of(s_buf), store, weights.at[2], bond_buf.at[2], groups, 8)

    def y_copy(g, c):
        return pltpu.make_async_copy(
            y_buf.at[c, g], out_ref.at[pl.ds(pl.multiple_of(g * lanes, lanes), lanes), c, :], y_sem.at[c, g]
        )

    def store_y(g, value):
        for c in range(2):
            y_buf[c, g] = value[:, c * lanes : (c + 1) * lanes]
            y_copy(g, c).start()

    apply_gate(parts_of(f_buf), store_y, weights.at[3], bond_buf.at[3], groups, 8)
    for g in range(groups):
        for c in range(2):
            y_copy(g, c).wait()


def launch(body, scalars, ins, out_shape, scratch, steps, dim, work, limit=VMEM_LIMIT):
    anywhere = pl.BlockSpec(memory_space=pl.ANY)
    scratch, sems = scratch
    common = [
        pltpu.VMEM((steps, 2, dim, dim), jnp.bfloat16),
        pltpu.VMEM((steps, 2, dim), jnp.float32),
        pltpu.VMEM((2, dim, dim), jnp.float32),
        pltpu.VMEM((steps, 2 * dim, 2 * dim), jnp.bfloat16),
        pltpu.SemaphoreType.DMA((steps, 2)),
    ]
    return pl.pallas_call(
        body,
        out_shape=[jax.ShapeDtypeStruct(shape, jnp.float32) for shape in out_shape],
        grid_spec=pltpu.PrefetchScalarGridSpec(
            num_scalar_prefetch=2,
            grid=(1,),
            in_specs=[anywhere] * len(ins),
            out_specs=[anywhere] * len(out_shape),
            scratch_shapes=[pltpu.VMEM(shape, jnp.float32) for shape in scratch]
            + common
            + [pltpu.SemaphoreType.DMA(shape) for shape in sems],
        ),
        compiler_params=pltpu.CompilerParams(vmem_limit_bytes=limit),
        cost_estimate=pl.CostEstimate(flops=work * 4 * dim**4, bytes_accessed=0, transcendentals=0),
    )(*scalars, *ins)


def swap(piece, axis, k):
    n = lax.axis_size(axis)
    return lax.ppermute(piece, axis, [(i, i ^ k) for i in range(n)])


def fast_body(state, gates, bonds, order, bits):
    dim = gates.shape[-1]
    rows = state.shape[1] // dim
    m = rows // dim
    n = lax.axis_size("outer")
    half = n // 2
    scalars = (order, bits)
    x = state.reshape(2, rows, dim).transpose(1, 0, 2).reshape(dim, m, 2, dim)
    piece = (2, m // n, dim, dim)
    block = (2, m, dim // 2, dim)
    mids = [block, (2, m // 2, dim, dim)]
    *far, near = launch(
        functools.partial(head_kernel, n=n),
        scalars,
        (x, gates, bonds),
        [piece] * half + [(rows, dim)],
        ([(2, m, dim, dim), (rows, dim), (rows, dim)] + mids, [(2, m), (half,), ()]),
        3,
        dim,
        8,
        None,
    )
    sent = []
    for k in range(half):
        sent.append(swap(far[k], "outer", half + k))
    far = sent
    near = launch(
        functools.partial(near_kernel, n=n),
        scalars,
        (near, gates, bonds),
        [piece] * half,
        ([(rows, dim)] + mids, [(half,), ()]),
        2,
        dim,
        4,
    )
    near = [near[0]] + [swap(near[k], "outer", k) for k in range(1, half)]
    own, other = launch(
        functools.partial(join_kernel, n=n),
        scalars,
        (gates, bonds, *near, *far),
        [block, block],
        ([(2, m, dim, dim), block, block], [(n,), (2, 2)]),
        1,
        dim,
        4,
    )
    got = swap(other, "inner", 1)
    done = launch(
        own_kernel, scalars, (own, gates, bonds), [mids[1]], ([block, block, mids[1]], [(), ()]), 2, dim, 4
    )[0]
    out = launch(
        tail_kernel,
        scalars,
        (done, got, gates, bonds),
        [(rows, 2, dim)],
        ([block, block, (2, m, dim, dim), (2, m, dim, dim), (2, m, dim, dim)], [(2,), (2, m)]),
        4,
        dim,
        12,
    )[0]
    return out.transpose(1, 0, 2).reshape(2, rows * dim)


def body(state, gates, bonds, order, bits):
    dim = gates.shape[-1]
    m = state.shape[1] // dim // dim
    n = lax.axis_size("outer")
    if lax.axis_size("inner") == 2 and m * 8 == dim and m % n == 0:
        return fast_body(state, gates, bonds, order, bits)
    return general_body(state, gates, bonds, order, bits)


def solution(mesh):
    in_specs = (P(None, ("parts", "outer", "inner")), P(), P(), P(), P("parts"))
    out_specs = P(None, ("parts", "outer", "inner"))
    return jax.shard_map(body, mesh=mesh, in_specs=in_specs, out_specs=out_specs, check_vma=False)
```

```python
import functools

import jax
import jax.numpy as jnp
from jax import lax
from jax.experimental import pallas as pl
from jax.experimental.pallas import tpu as pltpu
from jax.sharding import PartitionSpec as P


UNROLL = 8


def build_weights(gate_ref, weight_ref):
    dim = gate_ref.shape[-1]
    real = gate_ref[0, 0].astype(jnp.float32).T.astype(jnp.bfloat16)
    imag = gate_ref[0, 1].astype(jnp.float32).T.astype(jnp.bfloat16)
    weight_ref[:dim, :dim] = real
    weight_ref[:dim, dim:] = imag
    weight_ref[dim:, :dim] = -imag
    weight_ref[dim:, dim:] = real


def contract(load, store, weight_ref, bond_ref, groups):
    bond_real = bond_ref[0, 0, 0:1, :]
    bond_imag = bond_ref[0, 0, 1:2, :]
    unroll = min(UNROLL, groups)

    def some(index, carry):
        high, low = [], []
        for k in range(unroll):
            real, imag = load(index * unroll + k)
            real, imag = real.T, imag.T
            scaled = jnp.concatenate(
                [real * bond_real - imag * bond_imag, real * bond_imag + imag * bond_real], axis=1
            )
            head = scaled.astype(jnp.bfloat16)
            high.append(head)
            low.append((scaled - head.astype(jnp.float32)).astype(jnp.bfloat16))
        product = jnp.dot(
            jnp.concatenate(high + low, axis=0), weight_ref[...], preferred_element_type=jnp.float32
        )
        half = product.shape[0] // 2
        product = product[:half] + product[half:]
        size = half // unroll
        for k in range(unroll):
            store(index * unroll + k, product[k * size : (k + 1) * size])
        return carry

    lax.fori_loop(0, groups // unroll, some, 0)


def kernel(order_ref, bits_ref, *refs, steps, n_in, n_out, in_axis, out_axis, rows):
    del order_ref, bits_ref
    refs = list(refs)
    ins = [refs.pop(0) for _ in range(n_in)]
    gates = [refs.pop(0) for _ in range(steps)]
    bonds = [refs.pop(0) for _ in range(steps)]
    outs = [refs.pop(0) for _ in range(n_out)]
    weight_ref, bufs, in_sem, out_sem = refs
    dim = weight_ref.shape[-1] // 2
    groups = rows // dim

    if in_axis is not None:
        me = lax.axis_index(in_axis)
        part = rows // n_in
        copies = []
        for k in range(n_in):
            start = pl.multiple_of(lax.rem(me + (n_in - k), n_in) * part, part)
            for c in range(2):
                copies.append(
                    pltpu.make_async_copy(
                        ins[k].at[c], bufs.at[0, c, pl.ds(start, part), :], in_sem.at[k, c]
                    )
                )
                copies[-1].start()

    for s in range(steps):
        build_weights(gates[s], weight_ref.at[s])
    if in_axis is not None:
        for copy in copies:
            copy.wait()

    def load_interleaved(g):
        return tuple(ins[0][pl.ds(2 * g + c, dim, stride=2 * groups), :] for c in range(2))

    def loader(which):
        def load(g):
            return tuple(bufs[which, c, pl.ds(g, dim, stride=groups), :] for c in range(2))

        return load

    def storer(which):
        def store(g, value):
            for c in range(2):
                bufs[which, c, pl.ds(pl.multiple_of(g * dim, dim), dim), :] = value[
                    :, c * dim : (c + 1) * dim
                ]

        return store

    def store_interleaved(g, value):
        for c in range(2):
            outs[0][pl.ds(2 * g * dim + c, dim, stride=2), :] = value[:, c * dim : (c + 1) * dim]

    for s in range(steps):
        load = load_interleaved if in_axis is None and s == 0 else loader(s % 2)
        last = out_axis is None and s == steps - 1
        store = store_interleaved if last else storer((s + 1) % 2)
        contract(load, store, weight_ref.at[s], bonds[s], groups)

    if out_axis is not None:
        me = lax.axis_index(out_axis)
        part = rows // n_out
        copies = []
        for k in range(n_out):
            start = pl.multiple_of(lax.rem(me + k, n_out) * part, part)
            for c in range(2):
                copies.append(
                    pltpu.make_async_copy(
                        bufs.at[steps % 2, c, pl.ds(start, part), :], outs[k].at[c], out_sem.at[k, c]
                    )
                )
                copies[-1].start()
        for copy in copies:
            copy.wait()


def call(ins, gates, bonds, order, bits, first, steps, rows, n_out, in_axis, out_axis):
    dim = gates.shape[-1]
    n_in = len(ins)

    def gate_map(k, i, order, bits):
        return (order[first + k], 0, 0, 0)

    def bond_map(k, i, order, bits):
        return (order[first + k], bits[first + k], 0, 0)

    anywhere = pl.BlockSpec(memory_space=pl.ANY)
    flat = pl.BlockSpec((2 * rows, dim), lambda i, order, bits: (0, 0))
    in_specs = [flat] if in_axis is None else [anywhere] * n_in
    in_specs += [
        pl.BlockSpec((1,) + gates.shape[1:], functools.partial(gate_map, k)) for k in range(steps)
    ]
    in_specs += [
        pl.BlockSpec((1, 1) + bonds.shape[2:], functools.partial(bond_map, k)) for k in range(steps)
    ]
    if out_axis is None:
        out_shape = [jax.ShapeDtypeStruct((2 * rows, dim), jnp.float32)]
        out_specs = [flat]
    else:
        out_shape = [jax.ShapeDtypeStruct((2, rows // n_out, dim), jnp.float32)] * n_out
        out_specs = [anywhere] * n_out
    return pl.pallas_call(
        functools.partial(
            kernel,
            steps=steps,
            n_in=n_in,
            n_out=n_out,
            in_axis=in_axis,
            out_axis=out_axis,
            rows=rows,
        ),
        out_shape=out_shape,
        grid_spec=pltpu.PrefetchScalarGridSpec(
            num_scalar_prefetch=2,
            grid=(1,),
            in_specs=in_specs,
            out_specs=out_specs,
            scratch_shapes=[
                pltpu.VMEM((steps, 2 * dim, 2 * dim), jnp.bfloat16),
                pltpu.VMEM((2, 2, rows, dim), jnp.float32),
                pltpu.SemaphoreType.DMA((n_in, 2)),
                pltpu.SemaphoreType.DMA((n_out, 2)),
            ],
        ),
        cost_estimate=pl.CostEstimate(
            flops=steps * 16 * rows * dim * dim, bytes_accessed=16 * rows * dim, transcendentals=0
        ),
    )(order, bits, *ins, *([gates] * steps), *([bonds] * steps))


def exchange(pieces, axis):
    n = len(pieces)
    return [pieces[0]] + [
        lax.ppermute(pieces[k], axis, [(i, (i + k) % n) for i in range(n)]) for k in range(1, n)
    ]


def general_body(state, gates, bonds, order, bits):
    dim = gates.shape[-1]
    rows = state.shape[1] // dim
    leading = lax.axis_size("outer")
    second = lax.axis_size("inner")
    flat = state.reshape(2, rows, dim).transpose(1, 0, 2).reshape(2 * rows, dim)
    run = functools.partial(call, gates=gates, bonds=bonds, order=order, bits=bits, rows=rows)
    pieces = run([flat], first=0, steps=3, n_out=leading, in_axis=None, out_axis="outer")
    pieces = exchange(pieces, "outer")
    pieces = run(pieces, first=3, steps=3, n_out=second, in_axis="outer", out_axis="inner")
    pieces = exchange(pieces, "inner")
    (flat,) = run(pieces, first=6, steps=2, n_out=1, in_axis="inner", out_axis=None)
    return flat.reshape(rows, 2, dim).transpose(1, 0, 2).reshape(2, rows * dim)


DOT_ROWS = 128
TAIL_BATCHES = 2
VMEM_LIMIT = 20 * 2**20


def gate_rows(gate_ref, scratch_ref, order):
    for c in range(2):
        scratch_ref[c] = gate_ref[c].astype(jnp.float32)
    if order is None:
        return [scratch_ref[c] for c in range(2)]
    tall = scratch_ref.shape[1] // len(order)
    return [
        jnp.concatenate([scratch_ref[c, pl.ds(t, tall, stride=len(order)), :] for t in order], axis=0)
        for c in range(2)
    ]


def swap_lanes(value, amount, steps):
    lane = lax.broadcasted_iota(jnp.int32, value.shape, 1)
    size = value.shape[1]
    for s in steps:
        other = jnp.where((lane & s) != 0, pltpu.roll(value, s, 1), pltpu.roll(value, size - s, 1))
        value = jnp.where((amount & s) != 0, other, value)
    return value


def make_weight(gate_ref, scratch_ref, weight_ref, order=None, halves=False, lanes=None):
    real, imag = gate_rows(gate_ref, scratch_ref, order)
    if lanes is not None:
        real, imag = swap_lanes(real, *lanes), swap_lanes(imag, *lanes)
    dim = real.shape[0]
    cut = [(0, dim // 2), (dim // 2, dim)] if halves else [(0, dim)]
    upper = [m[a:b] for a, b in cut for m in (real, imag)]
    lower = [m[a:b] for a, b in cut for m in (-imag, real)]
    weight_ref[:dim] = jnp.concatenate(upper, axis=0).T.astype(jnp.bfloat16)
    weight_ref[dim:] = jnp.concatenate(lower, axis=0).T.astype(jnp.bfloat16)


def apply_gate(load, store, weight_ref, bond_ref, groups, before=None, after=None, batch=None):
    bond_real = bond_ref[0:1, :]
    bond_imag = bond_ref[1:2, :]
    batch = batch or groups
    for first in range(0, groups, batch):
        if before is not None:
            before(range(first, first + batch))
        held = []
        for g in range(first, first + batch):
            tiles = load(g)
            if len(tiles) == 1:
                both = tiles[0].T
                half = both.shape[0] // 2
                real, imag = both[:half], both[half:]
            else:
                real, imag = tiles[0].T, tiles[1].T
            scaled = jnp.concatenate(
                [real * bond_real - imag * bond_imag, real * bond_imag + imag * bond_real], axis=1
            )
            head = scaled.astype(jnp.bfloat16)
            held.append((g, head, (scaled - head.astype(jnp.float32)).astype(jnp.bfloat16)))
            rows = scaled.shape[0]
            if rows * len(held) < DOT_ROWS and g + 1 < first + batch:
                continue
            lhs = jnp.concatenate([h for _, h, _ in held] + [l for _, _, l in held], axis=0)
            product = jnp.dot(lhs, weight_ref[...], preferred_element_type=jnp.float32)
            half = product.shape[0] // 2
            product = product[:half] + product[half:]
            for k, (at, _, _) in enumerate(held):
                store(at, product[k * rows : (k + 1) * rows])
            held = []
        if after is not None:
            after(range(first, first + batch))


def tiles_of(ref, lead=()):
    def load(g):
        value = ref[(*lead, slice(None), pl.ds(g * 8, 8), slice(None))]
        return value.reshape(-1, value.shape[-1])

    return load


def parts_of(ref):
    loads = [tiles_of(ref, (c,)) for c in range(2)]
    return lambda g: [load(g) for load in loads]


def fetch(order_ref, bits_ref, first, gates_ref, bonds_ref, gate_buf, bond_buf, sem):
    copies = []
    for k in range(gate_buf.shape[0]):
        which = order_ref[first + k]
        copies.append(pltpu.make_async_copy(gates_ref.at[which], gate_buf.at[k], sem.at[k, 0]))
        copies.append(
            pltpu.make_async_copy(bonds_ref.at[which, bits_ref[first + k]], bond_buf.at[k], sem.at[k, 1])
        )
    for copy in copies:
        copy.start()
    return copies


def start_all(copies):
    for copy in copies:
        copy.start()
    return copies


def wait_all(copies):
    for copy in copies:
        copy.wait()


def second_third(half, d1, out_buf, targets, weights, bonds):
    groups = d1.shape[1]
    lanes = half.shape[1]

    def load(g):
        return [half[pl.ds(g, lanes, stride=groups), :]]

    def store(g, value):
        for c in range(2):
            d1[c, g] = value[:, c * lanes : (c + 1) * lanes]

    apply_gate(load, store, weights.at[0], bonds.at[0], groups)

    def store_out(g, value):
        for c in range(2):
            out_buf[c, g] = value[:, c * lanes : (c + 1) * lanes]

    apply_gate(parts_of(d1), store_out, weights.at[1], bonds.at[1], out_buf.shape[1])
    wait_all(start_all(targets))


def head_kernel(order_ref, bits_ref, x_ref, gates_ref, bonds_ref, *refs, n):
    far_outs, near_ref = refs[:n], refs[n]
    x_buf, far, near, d1, out_buf, gate_buf, bond_buf, gate_rows_buf, weights, g_sem, x_sem, o_sem, n_sem = refs[
        n + 1 :
    ]
    groups = x_buf.shape[1]
    me = lax.axis_index("outer")
    gate_copies = fetch(order_ref, bits_ref, 0, gates_ref, bonds_ref, gate_buf, bond_buf, g_sem)

    def x_copy(g, c):
        return pltpu.make_async_copy(x_ref.at[:, g, c, :], x_buf.at[c, g], x_sem.at[c, g])

    for g in range(groups):
        for c in range(2):
            x_copy(g, c).start()
    wait_all(gate_copies)
    rest = groups // n
    leads = [(me ^ k) * rest + r for k in [*range(n // 2, n), *range(n // 2)] for r in range(rest)]
    tiles = list(range(groups))
    make_weight(gate_buf.at[0], gate_rows_buf, weights.at[0], leads, True)
    make_weight(gate_buf.at[1], gate_rows_buf, weights.at[1], tiles)
    make_weight(gate_buf.at[2], gate_rows_buf, weights.at[2], tiles, True)

    def load(g):
        return [x_buf[c, g] for c in range(2)]

    def arrive(some):
        wait_all([x_copy(g, c) for g in some for c in range(2)])

    def store(g, value):
        lanes = far.shape[1]
        rows = pl.ds(g * lanes, lanes)
        far[rows, :] = value[:, :lanes]
        near[rows, :] = value[:, lanes:]

    apply_gate(load, store, weights.at[0], bond_buf.at[0], groups, before=arrive)
    near_copy = pltpu.make_async_copy(near, near_ref, n_sem)
    near_copy.start()
    targets = [
        pltpu.make_async_copy(out_buf.at[chunk, pl.ds(k * rest, rest)], far_outs[2 * k + chunk], o_sem.at[k, chunk])
        for chunk in range(2)
        for k in range(n // 2)
    ]
    second_third(far, d1, out_buf, targets, weights.at[pl.ds(1, 2)], bond_buf.at[pl.ds(1, 2)])
    near_copy.wait()


def near_kernel(order_ref, bits_ref, near_ref, gates_ref, bonds_ref, *refs, n):
    outs = refs[: n // 2]
    near, d1, out_buf, gate_buf, bond_buf, gate_rows_buf, weights, g_sem, o_sem, n_sem = refs[n // 2 :]
    near_copy = pltpu.make_async_copy(near_ref, near, n_sem)
    near_copy.start()
    wait_all(fetch(order_ref, bits_ref, 1, gates_ref, bonds_ref, gate_buf, bond_buf, g_sem))
    tiles = list(range(d1.shape[1]))
    make_weight(gate_buf.at[0], gate_rows_buf, weights.at[0], tiles)
    make_weight(gate_buf.at[1], gate_rows_buf, weights.at[1], tiles, True)
    near_copy.wait()
    rest = d1.shape[1] // n
    targets = [
        pltpu.make_async_copy(out_buf.at[:, pl.ds(k * rest, rest)], outs[k], o_sem.at[k]) for k in range(n // 2)
    ]
    second_third(near, d1, out_buf, targets, weights, bond_buf)


def prep_kernel(order_ref, bits_ref, gates_ref, bonds_ref, weights, bonds, gate_buf, bond_buf, gate_rows_buf, g_sem, *, n):
    me = lax.axis_index("outer")
    core = lax.axis_index("inner")
    wait_all(fetch(order_ref, bits_ref, 3, gates_ref, bonds_ref, gate_buf, bond_buf, g_sem))
    dim = gate_rows_buf.shape[-1]
    groups = dim // 8
    tiles = list(range(groups))
    leads = [(core ^ j) * (groups // 2) + r for j in range(2) for r in range(groups // 2)]
    part = dim // n
    joined = (me * part, [part << i for i in range((n - 1).bit_length())])
    cored = (core * (dim // 2), [dim // 2])
    make_weight(gate_buf.at[0], gate_rows_buf, weights.at[0], leads, True, joined)
    make_weight(gate_buf.at[1], gate_rows_buf, weights.at[1], tiles)
    make_weight(gate_buf.at[2], gate_rows_buf, weights.at[2], tiles)
    make_weight(gate_buf.at[3], gate_rows_buf, weights.at[3], None, False, cored)
    make_weight(gate_buf.at[4], gate_rows_buf, weights.at[4])
    for k, lanes in enumerate([joined, None, None, cored, None]):
        bonds[k] = bond_buf[k] if lanes is None else swap_lanes(bond_buf[k], *lanes)


def halves(ref):
    def store(g, value):
        lanes = value.shape[1] // 2
        for c in range(2):
            ref[c, g] = value[:, c * lanes : (c + 1) * lanes]

    return store


def stacked(refs, c):
    def load(g):
        values = [ref[(*lead, slice(None), pl.ds(g * 8, 8), slice(None))] for ref, lead in refs(c)]
        value = jnp.concatenate(values, axis=0)
        return value.reshape(-1, value.shape[-1])

    return load


def pair_of(refs):
    loads = [stacked(refs, c) for c in range(2)]
    return lambda g: [load(g) for load in loads]


def join_kernel(weights, bonds, *refs, n, chunk):
    near, far, (own, other) = refs[: n // 2], refs[n // 2 : n], refs[n:]
    groups = own.shape[0]
    load = stacked(lambda c: [(r, (chunk,)) for r in near] + [(r, ()) for r in far], 0)

    def store(g, value):
        lanes = own.shape[-1]
        own[g] = value[:, :lanes]
        other[g] = value[:, lanes:]

    apply_gate(lambda g: [load(g)], store, weights.at[0], bonds.at[0], groups)


def fifth(q, e, weights, bonds):
    load = tiles_of(q)
    apply_gate(lambda g: [load(g)], halves(e), weights.at[1], bonds.at[1], q.shape[1] // 8)


def sixth(e0, e1, s, weights, bonds):
    load = pair_of(lambda c: [(e0, (c,)), (e1, (c,))])
    apply_gate(load, halves(s), weights.at[2], bonds.at[2], s.shape[1])


def fifth_kernel(weights, bonds, q, e):
    fifth(q, e, weights, bonds)


def own_kernel(weights, bonds, e0, q1, s, e1):
    fifth(q1, e1, weights, bonds)
    sixth(e0, e1, s, weights, bonds)


def tail_kernel(weights, bonds, s_own, e0, q1, out_ref, e1, s_got, f, y, y_sem):
    fifth(q1, e1, weights, bonds)
    sixth(e0, e1, s_got, weights, bonds)
    groups = f.shape[1]
    lanes = f.shape[-1]
    apply_gate(pair_of(lambda c: [(s_own, (c,)), (s_got, (c,))]), halves(f), weights.at[3], bonds.at[3], groups)

    def y_copy(g, c):
        return pltpu.make_async_copy(
            y.at[c, g], out_ref.at[pl.ds(g * lanes, lanes), c, :], y_sem.at[c, g]
        )

    def leave(some):
        start_all([y_copy(g, c) for g in some for c in range(2)])

    apply_gate(
        parts_of(f), halves(y), weights.at[4], bonds.at[4], groups, after=leave, batch=groups // TAIL_BATCHES
    )
    wait_all([y_copy(g, c) for g in range(groups) for c in range(2)])


def inside(body, ins, outs, scratch=(), work=4, out_specs=None):
    here = pl.BlockSpec(memory_space=pltpu.VMEM)
    dim = ins[0].shape[-1] // 2
    return pl.pallas_call(
        body,
        out_shape=[jax.ShapeDtypeStruct(shape, jnp.float32) for shape in outs],
        in_specs=[here] * len(ins),
        out_specs=out_specs or [here] * len(outs),
        scratch_shapes=list(scratch),
        compiler_params=pltpu.CompilerParams(vmem_limit_bytes=VMEM_LIMIT),
        cost_estimate=pl.CostEstimate(flops=work * 4 * dim**4, bytes_accessed=0, transcendentals=0),
    )(*ins)


def launch(body, scalars, ins, out_shape, scratch, steps, dim, work, limit=VMEM_LIMIT):
    anywhere = pl.BlockSpec(memory_space=pl.ANY)
    scratch, sems = scratch
    common = [
        pltpu.VMEM((steps, 2, dim, dim), jnp.bfloat16),
        pltpu.VMEM((steps, 2, dim), jnp.float32),
        pltpu.VMEM((2, dim, dim), jnp.float32),
        pltpu.VMEM((steps, 2 * dim, 2 * dim), jnp.bfloat16),
        pltpu.SemaphoreType.DMA((steps, 2)),
    ]
    return pl.pallas_call(
        body,
        out_shape=[jax.ShapeDtypeStruct(shape, jnp.float32) for shape in out_shape],
        grid_spec=pltpu.PrefetchScalarGridSpec(
            num_scalar_prefetch=2,
            grid=(1,),
            in_specs=[anywhere] * len(ins),
            out_specs=[anywhere] * len(out_shape),
            scratch_shapes=[pltpu.VMEM(shape, jnp.float32) for shape in scratch]
            + common
            + [pltpu.SemaphoreType.DMA(shape) for shape in sems],
        ),
        compiler_params=pltpu.CompilerParams(vmem_limit_bytes=limit),
        cost_estimate=pl.CostEstimate(flops=work * 4 * dim**4, bytes_accessed=0, transcendentals=0),
    )(*scalars, *ins)


def prepare(scalars, gates, bonds, n):
    dim = gates.shape[-1]
    anywhere = pl.BlockSpec(memory_space=pl.ANY)
    here = pl.BlockSpec(memory_space=pltpu.VMEM)
    return pl.pallas_call(
        functools.partial(prep_kernel, n=n),
        out_shape=[
            jax.ShapeDtypeStruct((5, 2 * dim, 2 * dim), jnp.bfloat16),
            jax.ShapeDtypeStruct((5, 2, dim), jnp.float32),
        ],
        grid_spec=pltpu.PrefetchScalarGridSpec(
            num_scalar_prefetch=2,
            grid=(),
            in_specs=[anywhere] * 2,
            out_specs=[here] * 2,
            scratch_shapes=[
                pltpu.VMEM((5, 2, dim, dim), jnp.bfloat16),
                pltpu.VMEM((5, 2, dim), jnp.float32),
                pltpu.VMEM((2, dim, dim), jnp.float32),
                pltpu.SemaphoreType.DMA((5, 2)),
            ],
        ),
        compiler_params=pltpu.CompilerParams(vmem_limit_bytes=VMEM_LIMIT),
        cost_estimate=pl.CostEstimate(flops=4 * dim**4, bytes_accessed=0, transcendentals=0),
    )(*scalars, gates, bonds)


def swap(piece, axis, k):
    n = lax.axis_size(axis)
    return lax.ppermute(piece, axis, [(i, i ^ k) for i in range(n)])


def fast_body(state, gates, bonds, order, bits):
    dim = gates.shape[-1]
    rows = state.shape[1] // dim
    m = rows // dim
    n = lax.axis_size("outer")
    half = n // 2
    scalars = (order, bits)
    x = state.reshape(2, rows, dim).transpose(1, 0, 2).reshape(dim, m, 2, dim)
    piece = (2, m // n, dim, dim)
    block = (2, m, dim // 2, dim)
    mids = [block, (2, m // 2, dim, dim)]
    *far, near = launch(
        functools.partial(head_kernel, n=n),
        scalars,
        (x, gates, bonds),
        [piece[1:]] * n + [(rows, dim)],
        ([(2, m, dim, dim), (rows, dim), (rows, dim)] + mids, [(2, m), (half, 2), ()]),
        3,
        dim,
        8,
        None,
    )
    sent = []
    for chunk in range(2):
        for k in range(half):
            sent.append(swap(far[2 * k + chunk], "outer", half + k))
    near = launch(
        functools.partial(near_kernel, n=n),
        scalars,
        (near, gates, bonds),
        [piece] * half,
        ([(rows, dim)] + mids, [(half,), ()]),
        2,
        dim,
        4,
    )
    near = [near[0]] + [swap(near[k], "outer", k) for k in range(1, half)]
    prepared = prepare(scalars, gates, bonds, n)
    q = (m, dim // 2, dim)
    e = (2, m // 2, dim // 2, dim)
    e_buf = pltpu.VMEM(e, jnp.float32)
    s = mids[1]
    joined = []
    for chunk in range(2):
        joined.append(
            inside(
                functools.partial(join_kernel, n=n, chunk=chunk),
                [*prepared, *near, *sent[chunk * half : (chunk + 1) * half]],
                [q, q],
                work=2,
            )
        )
    own, other = zip(*joined)
    got = []
    for chunk in range(2):
        got.append(swap(other[chunk], "inner", 1))
    e_own = inside(fifth_kernel, [*prepared, own[0]], [e], work=1)[0]
    e_got = inside(fifth_kernel, [*prepared, got[0]], [e], work=1)[0]
    s_own = inside(own_kernel, [*prepared, e_own, own[1]], [s], [e_buf], work=3)[0]
    full = pltpu.VMEM((2, m, dim, dim), jnp.float32)
    out = inside(
        tail_kernel,
        [*prepared, s_own, e_got, got[1]],
        [(rows, 2, dim)],
        [e_buf, pltpu.VMEM(s, jnp.float32), full, full, pltpu.SemaphoreType.DMA((2, m))],
        work=12,
        out_specs=[pl.BlockSpec(memory_space=pl.ANY)],
    )[0]
    return out.transpose(1, 0, 2).reshape(2, rows * dim)


def body(state, gates, bonds, order, bits):
    dim = gates.shape[-1]
    m = state.shape[1] // dim // dim
    n = lax.axis_size("outer")
    if lax.axis_size("inner") == 2 and m * 8 == dim and m % n == 0:
        return fast_body(state, gates, bonds, order, bits)
    return general_body(state, gates, bonds, order, bits)


def solution(mesh):
    in_specs = (P(None, ("parts", "outer", "inner")), P(), P(), P(), P("parts"))
    out_specs = P(None, ("parts", "outer", "inner"))
    return jax.shard_map(body, mesh=mesh, in_specs=in_specs, out_specs=out_specs, check_vma=False)
```
